32 devices in a mesh: shard: 2 (over x), ctx: 4 (over z), tp: 4 (over y, core).
Axes of the slice: x: 2, y: 2, z: 4, core: 2. Of those that a mesh axis runs over, the one named last changes fastest.
Arguments:
- tokens: bfloat16 [6, 1024, 1152], P('shard', 'ctx'), may hold values from -6 to 6
- condition: bfloat16 [6, 1152], P('shard'), may hold values from -6 to 6
- ada_weight: bfloat16 [1152, 6912], P('shard'), may hold values from -0.1875 to 0.1875
- ada_bias: float32 [6912], replicated, may hold values from -3 to 3
- qkv_weight: bfloat16 [1152, 16, 216], P('shard', 'tp'), may hold values from -0.1875 to 0.1875
- qv_bias: float32 [16, 144], P('tp'), may hold values from -2 to 2
- out_weight: bfloat16 [1152, 1152], P('tp', 'shard'), may hold values from -1 to 1
- out_bias: float32 [1152], replicated, may hold values from -2 to 2
- up_weight: bfloat16 [1152, 4608], P('shard', 'tp'), may hold values from -0.1875 to 0.1875
- up_bias: float32 [4608], P('tp'), may hold values from -3 to 3
- down_weight: bfloat16 [4608, 1152], P('tp', 'shard'), may hold values from -0.09375 to 0.09375
- down_bias: float32 [1152], replicated, may hold values from -2 to 2
- cotangent: bfloat16 [6, 1024, 1152], P('shard', 'ctx'), may hold values from -6 to 6
Outputs:
- result: bfloat16 [6, 1024, 1152], P('shard', 'ctx')
- grad_tokens: float32 [6, 1024, 1152], P('shard', 'ctx')
- grad_condition: float32 [6, 1152], P('shard')
- grad_ada_weight: float32 [1152, 6912], P('shard')
- grad_ada_bias: float32 [6912], P('shard')
- grad_qkv_weight: float32 [1152, 16, 216], P('shard', 'tp')
- grad_qv_bias: float32 [16, 144], P('tp', 'shard')
- grad_out_weight: float32 [1152, 1152], P('tp', 'shard')
- grad_out_bias: float32 [1152], P('shard')
- grad_up_weight: float32 [1152, 4608], P('shard', 'tp')
- grad_up_bias: float32 [4608], P(('tp', 'shard'))
- grad_down_weight: float32 [4608, 1152], P('tp', 'shard')
- grad_down_bias: float32 [1152], P('shard')
The draws below stay inside these ranges and needn't reach their ends.
All inputs are finite; a program needn't handle non-finite values.
Results may differ from the reference program's by a relative error of at most 0.02.
The reference program's roundings to bfloat16 on the way count: a program that leaves them out, or rounds other values in their place, can miss the bound.
Values may be sent and summed in bfloat16 or wider, within the bound.
A program may use at most 192 MiB of HBM per device.

```python
import jax
import jax.numpy as jnp
from jax import lax

D = 1152
HEADS = 16
HD = 72
FF = 4608
SEQ = 1024
LATENTS = 6


def strengthened(values, stream_key, source, target, shards_of, factor):
    def block_of(dim):
        return (jnp.arange(values.shape[dim]) // (values.shape[dim] // shards_of)).reshape((-1,) + (1,) * (values.ndim - 1 - dim))

    first = jax.random.permutation(stream_key, shards_of)[block_of(target)]
    second = (block_of(target) + shards_of // 2) % shards_of
    return jnp.where((block_of(source) == first) | (block_of(source) == second), factor * values, values)


def levels(stream_key, shape, cuts, smallest, largest):
    gain = 1.0
    for dim, parts in cuts:
        draws = jax.random.uniform(jax.random.fold_in(jax.random.fold_in(stream_key, 6), dim), (parts,), jnp.float32, smallest / len(cuts), largest / len(cuts))
        gain = gain * jnp.repeat(jnp.exp(draws), shape[dim] // parts).reshape((-1,) + (1,) * (len(shape) - 1 - dim))
    return gain


def bell_draw(own_key, extent, spread, most, shards=(), kind=jnp.bfloat16):
    loudness = levels(own_key, extent, shards, -0.22, 0.18) if shards else 1.0
    result = jax.random.normal(own_key, extent, jnp.float32) * spread * loudness
    return jnp.minimum(jnp.maximum(result, -most), most).astype(kind)


def gaussian_with(rng, extent, deviation, bound, shards, heavy, held_as=jnp.bfloat16):
    array = deviation * jax.random.normal(rng, extent, jnp.float32)
    if shards:
        array = array * levels(rng, extent, shards, -0.22, 0.18)
    return jnp.clip(strengthened(array, jax.random.fold_in(rng, 3), *heavy), -bound, bound).astype(held_as)


def setup_inputs(seed: int = 0) -> dict:
    seeds = jax.random.split(jax.random.key(seed), 14)
    tokens = bell_draw(seeds[0], (LATENTS, SEQ, D), 1.0, 6.0, ((0, 2), (1, 4)))
    condition = bell_draw(seeds[1], (LATENTS, D), 1.0, 6.0, ((0, 2),))
    ada_weight = bell_draw(seeds[2], (D, 6 * D), D ** -0.5, 0.1875, ((0, 2),))
    ada_bias = bell_draw(seeds[3], (6 * D,), 0.5, 3.0, (), jnp.float32)
    qkv_weight = bell_draw(seeds[4], (D, HEADS, 3 * HD), D ** -0.5, 0.1875, ((0, 2), (1, 4)))
    qv_bias = bell_draw(seeds[5], (HEADS, 2 * HD), 0.3, 2.0, ((0, 4),), jnp.float32)
    out_weight = bell_draw(seeds[6], (D, D), (D // 32) ** -0.5, 1.0, ((0, 4), (1, 2)))
    out_bias = bell_draw(seeds[7], (D,), 0.3, 2.0, (), jnp.float32)
    up_weight = bell_draw(seeds[8], (D, FF), D ** -0.5, 0.1875, ((0, 2), (1, 4)))
    up_bias = bell_draw(seeds[9], (FF,), 0.5, 3.0, ((0, 4),), jnp.float32)
    down_weight = bell_draw(seeds[10], (FF, D), FF ** -0.5, 0.09375, ((0, 4), (1, 2)))
    down_bias = bell_draw(seeds[11], (D,), 0.3, 2.0, (), jnp.float32)
    cotangent = gaussian_with(seeds[12], (LATENTS, SEQ, D), 1.0, 6.0, ((0, 2), (1, 4)), (0, 2, 2, 2.0))
    return dict(tokens=tokens, condition=condition, ada_weight=ada_weight, ada_bias=ada_bias, qkv_weight=qkv_weight, qv_bias=qv_bias, out_weight=out_weight, out_bias=out_bias, up_weight=up_weight, up_bias=up_bias, down_weight=down_weight, down_bias=down_bias, cotangent=cotangent)


@jax.custom_vjp
def low(v):
    return lax.optimization_barrier(v.astype(jnp.bfloat16)).astype(jnp.float32)

@jax.custom_vjp
def low_back(v):
    return v

def low_keep(v):
    return (low(v), None)

def low_pass(kept, grad):
    return (grad,)

def back_keep(v):
    return (v, None)

def back_low(kept, grad):
    return (low(grad),)
low.defvjp(low_keep, low_pass)
low_back.defvjp(back_keep, back_low)
highest = lax.Precision.HIGHEST

def layer_norm(values):
    row_mean = lax.optimization_barrier(jnp.mean(values, -1, keepdims=True))
    centered = values - row_mean
    variance = lax.optimization_barrier(jnp.mean(centered * centered, -1, keepdims=True))
    return centered * lax.rsqrt(variance + 1e-06)

def gelu_tanh(values):
    return 0.5 * values * (1.0 + jnp.tanh(0.7978845608028654 * (values + 0.044715 * values * values * values)))

def diffusion_transformer_block(token_vector, condition_vector, parameter_bundle):
    ada_weight, ada_bias, qkv_weight, qv_bias, out_weight, out_bias, up_weight, up_bias, down_weight, down_bias = parameter_bundle
    model_width = token_vector.shape[1]
    head_count = qkv_weight.shape[1]
    head_size = qv_bias.shape[1] // 2
    cond_act = low(condition_vector * jax.nn.sigmoid(condition_vector))
    modulation = low_back(jnp.dot(cond_act, ada_weight, precision=highest)) + ada_bias
    modulation = modulation.reshape(6, model_width)
    normed = low(layer_norm(token_vector) * (1.0 + modulation[1]) + modulation[0])
    qkv_bias = jnp.concatenate([qv_bias[:, :head_size], jnp.zeros((head_count, head_size), jnp.float32), qv_bias[:, head_size:]], axis=1)
    qkv_rows = jnp.dot(normed, qkv_weight.reshape(model_width, -1), precision=highest).reshape(-1, head_count, 3 * head_size) + qkv_bias
    qkv_rows = low_back(low(qkv_rows))
    query_part = qkv_rows[:, :, :head_size]
    key_part = qkv_rows[:, :, head_size:2 * head_size]
    value_part = qkv_rows[:, :, 2 * head_size:]
    scores = low_back(jnp.einsum('shd,thd->hst', query_part, key_part, precision=highest) * head_size ** (-0.5))
    row_max = lax.optimization_barrier(jnp.max(scores, -1, keepdims=True))
    exponent = jnp.exp(scores - row_max)
    probability = low(exponent / lax.optimization_barrier(jnp.sum(exponent, -1, keepdims=True)))
    attended = jnp.einsum('hst,thd->shd', probability, value_part, precision=highest).reshape(-1, model_width)
    attended = low_back(low(attended))
    branch = low_back(jnp.dot(attended, out_weight, precision=highest)) + out_bias
    middle = token_vector + modulation[2] * branch
    normed_two = low(layer_norm(middle) * (1.0 + modulation[4]) + modulation[3])
    up_proj = low_back(jnp.dot(normed_two, up_weight, precision=highest)) + up_bias
    activated = low(gelu_tanh(up_proj))
    down_proj = low_back(jnp.dot(activated, down_weight, precision=highest)) + down_bias
    return middle + modulation[5] * down_proj

def reference(tokens, condition, ada_weight, ada_bias, qkv_weight, qv_bias, out_weight, out_bias, up_weight, up_bias, down_weight, down_bias, cotangent):
    parameters = (ada_weight.astype(jnp.float32), ada_bias.astype(jnp.float32), qkv_weight.astype(jnp.float32), qv_bias.astype(jnp.float32), out_weight.astype(jnp.float32), out_bias.astype(jnp.float32), up_weight.astype(jnp.float32), up_bias.astype(jnp.float32), down_weight.astype(jnp.float32), down_bias.astype(jnp.float32))

    def advance(totals, inputs):
        token_vector, condition_vector, grad_row = inputs
        block_output, backward_closure = jax.vjp(diffusion_transformer_block, token_vector, condition_vector, parameters)
        grad_tok, grad_cond, grad_params = backward_closure(grad_row)
        totals = jax.tree.map(lambda left, right: left + right, totals, grad_params)
        return (totals, (block_output.astype(jnp.bfloat16), grad_tok, grad_cond))
    initial = jax.tree.map(jnp.zeros_like, parameters)
    totals, stacked = lax.scan(advance, initial, (tokens.astype(jnp.float32), condition.astype(jnp.float32), cotangent.astype(jnp.float32)))
    outputs, grad_tokens, grad_condition = stacked
    return (outputs, grad_tokens, grad_condition, totals[0], totals[1], totals[2], totals[3], totals[4], totals[5], totals[6], totals[7], totals[8], totals[9])
```

```python
import jax
import jax.numpy as jnp
from jax import lax
from jax.sharding import PartitionSpec as P


def layer_norm(values):
    row_mean = jnp.mean(values, -1, keepdims=True)
    centered = values - row_mean
    variance = jnp.mean(centered * centered, -1, keepdims=True)
    return centered * lax.rsqrt(variance + 1e-06)


def modulate(values, shift_row, scale_row):
    return layer_norm(values) * (1.0 + scale_row[:, None, :]) + shift_row[:, None, :]


def gelu_tanh(values):
    return (
        0.5
        * values
        * (1.0 + jnp.tanh(0.7978845608028654 * (values + 0.044715 * values * values * values)))
    )


def silu_act(values):
    return values * jax.nn.sigmoid(values)


def contract_rows(left, right):
    return lax.dot_general(
        left, right, (((0,), (0,)), ((), ())), preferred_element_type=jnp.float32
    )


def contract_cols(left, right):
    return lax.dot_general(
        left, right, (((1,), (1,)), ((), ())), preferred_element_type=jnp.float32
    )


def attend_forward(packed):
    head_size = packed.shape[-1] // 3

    def one_latent(latent_qkv):
        query_part = latent_qkv[..., :head_size]
        key_part = latent_qkv[..., head_size : 2 * head_size]
        value_part = latent_qkv[..., 2 * head_size :]
        scores = jnp.einsum(
            "shd,thd->hst", query_part, key_part, preferred_element_type=jnp.float32
        ) * head_size ** (-0.5)
        row_max = jnp.max(scores, -1, keepdims=True)
        exponent = jnp.exp(scores - row_max)
        exp_total = jnp.sum(exponent, -1, keepdims=True)
        probability = (exponent / exp_total).astype(jnp.bfloat16)
        attended = jnp.einsum(
            "hst,thd->shd", probability, value_part, preferred_element_type=jnp.float32
        )
        log_total = (row_max + jnp.log(exp_total))[..., 0]
        return (attended.astype(jnp.bfloat16), log_total)

    attended, log_total = lax.map(one_latent, packed)
    return (attended, log_total, packed)


def attend_backward(inputs):
    latent_qkv, log_total, grad_out = inputs
    head_size = latent_qkv.shape[-1] // 3
    scale_factor = head_size ** (-0.5)
    query_part = latent_qkv[..., :head_size]
    key_part = latent_qkv[..., head_size : 2 * head_size]
    value_part = latent_qkv[..., 2 * head_size :]
    scores = (
        jnp.einsum("shd,thd->hst", query_part, key_part, preferred_element_type=jnp.float32)
        * scale_factor
    )
    probability = jnp.exp(scores - log_total[..., None])
    prob_low = probability.astype(jnp.bfloat16)
    grad_prob = jnp.einsum("shd,thd->hst", grad_out, value_part, preferred_element_type=jnp.float32)
    row_dot = jnp.sum(probability * grad_prob, -1, keepdims=True)
    grad_scores = (probability * (grad_prob - row_dot)).astype(jnp.bfloat16)
    grad_query = (
        jnp.einsum("hst,thd->shd", grad_scores, key_part, preferred_element_type=jnp.float32)
        * scale_factor
    )
    grad_key = (
        jnp.einsum("hst,shd->thd", grad_scores, query_part, preferred_element_type=jnp.float32)
        * scale_factor
    )
    grad_value = jnp.einsum("hst,shd->thd", prob_low, grad_out, preferred_element_type=jnp.float32)
    return jnp.concatenate([grad_query, grad_key, grad_value], -1).astype(jnp.bfloat16)


def swap(values, axis, distance):
    count = lax.axis_size(axis)
    return lax.ppermute(values, axis, [(i, i ^ distance) for i in range(count)])


def gather_shard(values, axis):
    if lax.axis_size("shard") != 2:
        return lax.all_gather(values, "shard", axis=axis, tiled=True)
    other = swap(values, "shard", 1)
    first = lax.axis_index("shard") == 0
    return jnp.concatenate(
        [jnp.where(first, values, other), jnp.where(first, other, values)], axis
    )


def scatter_shard(values, axis):
    count = lax.axis_size("shard")
    if count != 2:
        return lax.psum_scatter(
            values.astype(jnp.bfloat16), "shard", scatter_dimension=axis, tiled=True
        ).astype(jnp.float32)
    half = values.shape[axis] // 2
    low = lax.slice_in_dim(values, 0, half, axis=axis)
    high = lax.slice_in_dim(values, half, 2 * half, axis=axis)
    first = lax.axis_index("shard") == 0
    sent = jnp.where(first, high, low).astype(jnp.bfloat16)
    kept = jnp.where(first, low, high)
    return kept + swap(sent, "shard", 1).astype(jnp.float32)


def sum_axis(values, axis):
    count = lax.axis_size(axis)
    if count & (count - 1):
        return lax.psum(values, axis)
    distance = 1
    while distance < count:
        values = values + swap(values, axis, distance)
        distance *= 2
    return values


def local(
    tokens,
    condition,
    ada_weight,
    ada_bias,
    qkv_weight,
    qv_bias,
    out_weight,
    out_bias,
    up_weight,
    up_bias,
    down_weight,
    down_bias,
    cotangent,
):
    lat_count, local_len, model_width = tokens.shape
    head_local = qkv_weight.shape[1]
    head_size = qv_bias.shape[1] // 2
    row_count = lat_count * local_len
    shard_count = lax.axis_size("shard")
    shard_at = lax.axis_index("shard")
    stored = ada_weight.shape[0]
    cond_float = condition.astype(jnp.float32)
    cond_act = silu_act(cond_float).astype(jnp.bfloat16)
    cond_all = lax.all_gather(cond_act, "shard", axis=0, tiled=True) if shard_count != 2 else gather_shard(cond_act, 0)
    cond_mine = lax.dynamic_slice_in_dim(cond_all, shard_at * stored, stored, 1)
    mod_part = jnp.dot(cond_mine, ada_weight, preferred_element_type=jnp.float32)
    if shard_count == 2:
        first = shard_at == 0
        mod_low, mod_high = mod_part[:lat_count], mod_part[lat_count:]
        mod_raw = jnp.where(first, mod_low, mod_high) + swap(
            jnp.where(first, mod_high, mod_low), "shard", 1
        )
    else:
        mod_raw = lax.psum_scatter(mod_part, "shard", scatter_dimension=0, tiled=True)
    qkv_full = gather_shard(qkv_weight.reshape(stored, -1), 0)
    out_full = gather_shard(out_weight, 1)
    up_full = gather_shard(up_weight, 0)
    down_full = gather_shard(down_weight, 1)
    modulation = (mod_raw + ada_bias).reshape(lat_count, 6, model_width)
    tok_float = tokens.astype(jnp.float32)
    normed = (
        modulate(tok_float, modulation[:, 0], modulation[:, 1])
        .astype(jnp.bfloat16)
        .reshape(row_count, model_width)
    )
    qkv_bias = jnp.concatenate(
        [
            qv_bias[:, :head_size],
            jnp.zeros((head_local, head_size), jnp.float32),
            qv_bias[:, head_size:],
        ],
        1,
    )
    qkv_flat = qkv_full
    packed = jnp.dot(normed, qkv_flat, preferred_element_type=jnp.float32).reshape(
        lat_count, local_len, head_local, 3 * head_size
    )
    packed = (packed + qkv_bias).astype(jnp.bfloat16)
    attended, log_total, head_packed = attend_forward(
        lax.all_to_all(packed, "ctx", split_axis=2, concat_axis=1, tiled=True)
    )
    attn_rows = lax.all_to_all(attended, "ctx", split_axis=1, concat_axis=2, tiled=True).reshape(
        row_count, head_local * head_size
    )
    branch = (
        lax.psum(
            jnp.dot(attn_rows, out_full, preferred_element_type=jnp.float32).astype(jnp.bfloat16),
            "tp",
        ).astype(jnp.float32)
        + out_bias
    )
    branch = branch.reshape(lat_count, local_len, model_width)
    middle = tok_float + modulation[:, 2][:, None, :] * branch
    normed_two = (
        modulate(middle, modulation[:, 3], modulation[:, 4])
        .astype(jnp.bfloat16)
        .reshape(row_count, model_width)
    )
    up_proj = jnp.dot(normed_two, up_full, preferred_element_type=jnp.float32) + up_bias
    activated = gelu_tanh(up_proj).astype(jnp.bfloat16)
    down_proj = (
        lax.psum(
            jnp.dot(activated, down_full, preferred_element_type=jnp.float32).astype(jnp.bfloat16),
            "tp",
        ).astype(jnp.float32)
        + down_bias
    )
    down_proj = down_proj.reshape(lat_count, local_len, model_width)
    result = (middle + modulation[:, 5][:, None, :] * down_proj).astype(jnp.bfloat16)
    grad_out = cotangent.astype(jnp.float32)
    grad_gate2 = jnp.sum(grad_out * down_proj, 1)
    grad_down = grad_out * modulation[:, 5][:, None, :]
    grad_down_bias = jnp.sum(grad_down, (0, 1))
    grad_down_low = grad_down.astype(jnp.bfloat16).reshape(row_count, model_width)
    grad_act = contract_cols(grad_down_low, down_full)
    grad_down_weight = contract_rows(activated, grad_down_low)
    grad_up = jax.vjp(gelu_tanh, up_proj)[1](grad_act)[0]
    grad_up_bias = jnp.sum(grad_up, 0)
    grad_up_low = grad_up.astype(jnp.bfloat16)
    grad_up_weight = contract_rows(normed_two, grad_up_low)
    grad_normed_two = (
        lax.psum(contract_cols(grad_up_low, up_full).astype(jnp.bfloat16), "tp")
        .astype(jnp.float32)
        .reshape(lat_count, local_len, model_width)
    )
    pull_two = jax.vjp(modulate, middle, modulation[:, 3], modulation[:, 4])[1]
    grad_middle_norm, grad_shift2, grad_scale2 = pull_two(grad_normed_two)
    grad_middle = grad_out + grad_middle_norm
    grad_gate1 = jnp.sum(grad_middle * branch, 1)
    grad_branch = grad_middle * modulation[:, 2][:, None, :]
    grad_out_bias = jnp.sum(grad_branch, (0, 1))
    grad_branch_low = grad_branch.astype(jnp.bfloat16).reshape(row_count, model_width)
    grad_out_weight = contract_rows(attn_rows, grad_branch_low)
    grad_attended = (
        contract_cols(grad_branch_low, out_full)
        .astype(jnp.bfloat16)
        .reshape(lat_count, local_len, head_local, head_size)
    )
    grad_heads = lax.all_to_all(grad_attended, "ctx", split_axis=2, concat_axis=1, tiled=True)
    grad_packed_heads = lax.map(attend_backward, (head_packed, log_total, grad_heads))
    grad_packed = lax.all_to_all(grad_packed_heads, "ctx", split_axis=1, concat_axis=2, tiled=True)
    bias_sums = jnp.sum(grad_packed.astype(jnp.float32), (0, 1))
    grad_qv_bias = jnp.concatenate([bias_sums[:, :head_size], bias_sums[:, 2 * head_size :]], 1)
    grad_packed_rows = grad_packed.reshape(row_count, head_local * 3 * head_size)
    grad_qkv_weight = contract_rows(normed, grad_packed_rows)
    grad_normed = (
        lax.psum(contract_cols(grad_packed_rows, qkv_flat).astype(jnp.bfloat16), "tp")
        .astype(jnp.float32)
        .reshape(lat_count, local_len, model_width)
    )
    pull_one = jax.vjp(modulate, tok_float, modulation[:, 0], modulation[:, 1])[1]
    grad_tokens_norm, grad_shift1, grad_scale1 = pull_one(grad_normed)
    grad_tokens = grad_middle + grad_tokens_norm
    grad_mod_part = jnp.stack(
        [grad_shift1, grad_scale1, grad_gate1, grad_shift2, grad_scale2, grad_gate2], 1
    )
    small = jnp.concatenate(
        [
            grad_mod_part.reshape(-1),
            grad_qv_bias.reshape(-1),
            grad_out_bias,
            grad_up_bias,
            grad_down_bias,
        ]
    )
    small = sum_axis(small, "ctx")
    mod_count = lat_count * 6 * model_width
    grad_modulation = small[:mod_count].reshape(lat_count, 6 * model_width)
    bias_part = small[mod_count:]
    if shard_count == 2:
        other = swap(small, "shard", 1)
        other_mod = other[:mod_count].reshape(lat_count, 6 * model_width)
        grad_mod_all = jnp.concatenate(
            [
                jnp.where(first, grad_modulation, other_mod),
                jnp.where(first, other_mod, grad_modulation),
            ],
            0,
        )
        bias_all = bias_part + other[mod_count:]
    else:
        grad_mod_all = lax.all_gather(grad_modulation, "shard", axis=0, tiled=True)
        bias_all = lax.psum(bias_part, "shard")
    grad_ada_bias_all = jnp.sum(grad_mod_all, 0)
    grad_ada_bias = lax.dynamic_slice_in_dim(
        grad_ada_bias_all,
        shard_at * (6 * model_width // shard_count),
        6 * model_width // shard_count,
        0,
    )
    grad_mod_low = grad_mod_all.astype(jnp.bfloat16)
    grad_ada_weight = contract_rows(cond_mine, grad_mod_low)
    grad_cond_part = contract_cols(grad_mod_low, ada_weight)
    if shard_count == 2:
        part_low, part_high = grad_cond_part[:lat_count], grad_cond_part[lat_count:]
        kept = jnp.where(first, part_low, part_high)
        got = swap(jnp.where(first, part_high, part_low), "shard", 1)
        grad_cond_act = jnp.concatenate(
            [jnp.where(first, kept, got), jnp.where(first, got, kept)], 1
        )
    else:
        grad_cond_act = lax.all_to_all(
            grad_cond_part, "shard", split_axis=0, concat_axis=1, tiled=True
        )
    grad_condition = jax.vjp(silu_act, cond_float)[1](grad_cond_act)[0]

    def pick(values, start, size, axis):
        part = size // shard_count
        return lax.dynamic_slice_in_dim(
            values, start + shard_at * part, part, axis
        )

    bias_width = head_local * 2 * head_size
    hidden = grad_up_bias.shape[0]
    qv_sum = bias_all[:bias_width].reshape(head_local, 2 * head_size)
    summed = (
        lax.psum(scatter_shard(grad_qkv_weight, 0).astype(jnp.bfloat16), "ctx").astype(jnp.float32).reshape(stored, head_local, 3 * head_size),
        pick(qv_sum, 0, 2 * head_size, 1),
        lax.psum(scatter_shard(grad_out_weight, 1).astype(jnp.bfloat16), "ctx").astype(jnp.float32),
        pick(bias_all, bias_width, model_width, 0),
        lax.psum(scatter_shard(grad_up_weight, 0).astype(jnp.bfloat16), "ctx").astype(jnp.float32),
        pick(bias_all, bias_width + model_width, hidden, 0),
        lax.psum(scatter_shard(grad_down_weight, 1).astype(jnp.bfloat16), "ctx").astype(jnp.float32),
        pick(bias_all, bias_width + model_width + hidden, model_width, 0),
    )
    return (
        result,
        grad_tokens,
        grad_condition,
        grad_ada_weight,
        grad_ada_bias,
        summed[0],
        summed[1],
        summed[2],
        summed[3],
        summed[4],
        summed[5],
        summed[6],
        summed[7],
    )


def solution(mesh):
    return jax.shard_map(
        local,
        mesh=mesh,
        in_specs=(
            P("shard", "ctx", None),
            P("shard", None),
            P("shard", None),
            P(),
            P("shard", "tp", None),
            P("tp", None),
            P("tp", "shard"),
            P(),
            P("shard", "tp"),
            P("tp"),
            P("tp", "shard"),
            P(),
            P("shard", "ctx", None),
        ),
        out_specs=(
            P("shard", "ctx", None),
            P("shard", "ctx", None),
            P("shard", None),
            P("shard", None),
            P("shard"),
            P("shard", "tp", None),
            P("tp", "shard"),
            P("tp", "shard"),
            P("shard"),
            P("shard", "tp"),
            P(("tp", "shard")),
            P("tp", "shard"),
            P("shard"),
        ),
        check_vma=False,
    )
```
